128 devices in a mesh: prompt: 8 (over y, z_hi), sample: 16 (over x, z_lo, core).
Axes of the slice: x: 4, y: 4, z: 4 (z_hi: 2, z_lo: 2; z = z_hi * 2 + z_lo), core: 2. Of those that a mesh axis runs over, the one named last changes fastest.
Arguments:
- queries: bfloat16 [8, 128, 4096], P('prompt', 'sample'), may hold values from -250 to 250
- prompt_cache: bfloat16 [8, 16, 2048, 2048], P('prompt', 'sample'), may hold values from -6 to 6
- owner: int32 [8], P('prompt'), may hold values from 0 to 15
- prompt_len: int32 [8], P('prompt'), may hold values from 512 to 2048
- suffix_cache: bfloat16 [8, 128, 256, 2048], P('prompt', 'sample'), may hold values from -6 to 6
- suffix_len: int32 [8, 128], P('prompt', 'sample'), may hold values from 1 to 256
- new_kv: bfloat16 [8, 128, 2048], P('prompt', 'sample'), may hold values from -6 to 6
- out_weight: bfloat16 [4096, 4096], P(None, 'sample'), may hold values from -0.09375 to 0.09375
Outputs:
- mixed: bfloat16 [8, 128, 4096], P('prompt', None, 'sample')
The draws below stay inside these ranges and needn't reach their ends.
All inputs are finite; a program needn't handle non-finite values.
Results may differ from the reference program's by a relative error of at most 0.007.
Values may be sent and summed in bfloat16 or wider, within the bound.
No kernel may reach another device: no remote copies, remote signals or barrier semaphores. Data moves between devices by JAX's collectives and lax.ppermute only.
A program may use at most 192 MiB of HBM per device.

```python
import jax
import jax.numpy as jnp
from jax import lax

D = 4096
H = 32
KVH = 8
HD = 128
PLEN = 2048
SLEN = 256
PROMPTS = 8
SLOTS = 16
SAMPLES = 128
QW = 4096
KV2 = 2048
N_SAMPLE = 16


def shared_draw(key):
    key_cache, key_query = jax.random.split(jax.random.fold_in(key, 7))
    cache = jnp.clip(jax.random.normal(key_cache, (PROMPTS, SLOTS, PLEN, KV2), jnp.float32), -6.0, 6.0)
    queries = 0.5 * jnp.clip(jax.random.normal(key_query, (PROMPTS, SAMPLES, H * HD), jnp.float32), -6.0, 6.0)
    return (cache, queries)


def draw_queries(key, part):
    return shared_draw(key)[1].astype(jnp.bfloat16)


def draw_prompt_cache(key, part):
    return shared_draw(key)[0].astype(jnp.bfloat16)


def with_ends(values, rng, smallest, high):
    shape = values.shape
    spot = [jax.random.randint(jax.random.fold_in(rng, axis), (), 0, shape[axis]) for axis in range(len(shape))]
    values = values.at[tuple(spot)].set(smallest)
    longest = shape.index(max(shape))
    spot[longest] = (spot[longest] + 1) % shape[longest]
    return values.at[tuple(spot)].set(high)


def shard_levels(key, shape, cuts, smallest, largest):
    gain = 1.0
    for dim, blocks in cuts:
        steps = jax.random.uniform(jax.random.fold_in(jax.random.fold_in(key, 6), dim), (blocks,), jnp.float32, smallest / len(cuts), largest / len(cuts))
        gain = gain * jnp.repeat(jnp.exp(steps), shape[dim] // blocks).reshape((-1,) + (1,) * (len(shape) - 1 - dim))
    return gain


def noise(rng, shape, deviation, reach, cuts=(), kind=jnp.bfloat16):
    result = deviation * jax.random.normal(rng, shape, jnp.float32)
    if cuts:
        result = result * shard_levels(rng, shape, cuts, -0.22, 0.18)
    return jnp.clip(result, -reach, reach).astype(kind)


def setup_inputs(seed: int = 0) -> dict:
    streams_of = jax.random.split(jax.random.key(seed), 9)
    queries = draw_queries(jax.random.fold_in(streams_of[8], 71), 0)
    prompt_cache = draw_prompt_cache(jax.random.fold_in(streams_of[8], 71), 0)
    owner = with_ends(jax.random.randint(streams_of[2], (PROMPTS,), 0, N_SAMPLE), jax.random.fold_in(streams_of[2], 1), 0, N_SAMPLE - 1).astype(jnp.int32)
    prompt_len = with_ends(jax.random.randint(streams_of[3], (PROMPTS,), PLEN // 4, PLEN + 1), jax.random.fold_in(streams_of[3], 1), PLEN // 4, PLEN).astype(jnp.int32)
    suffix_cache = noise(streams_of[4], (PROMPTS, SAMPLES, SLEN, KV2), 1.0, 6.0, ((0, 8), (1, 16)))
    suffix_len = with_ends(jax.random.randint(streams_of[5], (PROMPTS, SAMPLES), 1, SLEN + 1), jax.random.fold_in(streams_of[5], 1), 1, SLEN).astype(jnp.int32)
    new_kv = noise(streams_of[6], (PROMPTS, SAMPLES, KV2), 1.0, 6.0, ((0, 8), (1, 16)))
    out_weight = noise(streams_of[7], (QW, D), QW ** -0.5, 0.09375, ((1, 16),))
    return {"queries": queries, "prompt_cache": prompt_cache, "owner": owner, "prompt_len": prompt_len, "suffix_cache": suffix_cache, "suffix_len": suffix_len, "new_kv": new_kv, "out_weight": out_weight}


def prefix_part(queries, cache, length):
    count = queries.shape[0]
    positions = cache.shape[0]
    query = queries.astype(jnp.float32).reshape(count, KVH, H // KVH, HD)
    keys = cache[:, :KVH * HD].astype(jnp.float32).reshape(positions, KVH, HD)
    values = cache[:, KVH * HD:].astype(jnp.float32).reshape(positions, KVH, HD)
    scores = jnp.einsum("sgjd,tgd->sgjt", query, keys) * (HD ** -0.5)
    valid = jnp.arange(positions, dtype=jnp.int32) < length
    scores = jnp.where(valid, scores, -1e30)
    top = jnp.max(scores, axis=-1)
    weights = jnp.exp(scores - top[..., None])
    total = jnp.sum(weights, axis=-1)
    rounded = weights.astype(jnp.bfloat16).astype(jnp.float32)
    output = jnp.einsum("sgjt,tgd->sgjd", rounded, values)
    return output.reshape(count, H, HD), top.reshape(count, H), total.reshape(count, H)


def suffix_part(queries, cache, lengths, own):
    count = queries.shape[0]
    positions = cache.shape[1]
    query = queries.astype(jnp.float32).reshape(count, KVH, H // KVH, HD)
    keys = cache[:, :, :KVH * HD].astype(jnp.float32).reshape(count, positions, KVH, HD)
    values = cache[:, :, KVH * HD:].astype(jnp.float32).reshape(count, positions, KVH, HD)
    own_key = own[:, :KVH * HD].astype(jnp.float32).reshape(count, KVH, HD)
    own_value = own[:, KVH * HD:].astype(jnp.float32).reshape(count, KVH, HD)
    scores = jnp.einsum("sgjd,stgd->sgjt", query, keys) * (HD ** -0.5)
    valid = jnp.arange(positions, dtype=jnp.int32)[None, :] < lengths[:, None]
    scores = jnp.where(valid[:, None, None, :], scores, -1e30)
    own_score = jnp.einsum("sgjd,sgd->sgj", query, own_key) * (HD ** -0.5)
    top = jnp.maximum(jnp.max(scores, axis=-1), own_score)
    weights = jnp.exp(scores - top[..., None])
    own_weight = jnp.exp(own_score - top)
    total = jnp.sum(weights, axis=-1) + own_weight
    rounded = weights.astype(jnp.bfloat16).astype(jnp.float32)
    output = jnp.einsum("sgjt,stgd->sgjd", rounded, values)
    own_rounded = own_weight.astype(jnp.bfloat16).astype(jnp.float32)
    output = output + own_rounded[..., None] * own_value[:, :, None, :]
    return output.reshape(count, H, HD), top.reshape(count, H), total.reshape(count, H)


def combine(prefix, suffix):
    out_pre, top_pre, total_pre = prefix
    out_suf, top_suf, total_suf = suffix
    top = jnp.maximum(top_pre, top_suf)
    factor_pre = jnp.exp(top_pre - top)
    factor_suf = jnp.exp(top_suf - top)
    numer = out_pre * factor_pre[..., None] + out_suf * factor_suf[..., None]
    denom = total_pre * factor_pre + total_suf * factor_suf
    attn = numer / denom[..., None]
    return attn.reshape(attn.shape[0], H * HD).astype(jnp.bfloat16)


def reference(queries, prompt_cache, owner, prompt_len, suffix_cache, suffix_len, new_kv, out_weight):
    def one_prompt(index):
        prefix = prefix_part(queries[index], prompt_cache[index, owner[index]], prompt_len[index])
        suffix = suffix_part(queries[index], suffix_cache[index], suffix_len[index], new_kv[index])
        attn = combine(prefix, suffix)
        return jnp.dot(attn, out_weight, preferred_element_type=jnp.float32).astype(jnp.bfloat16)

    return lax.map(one_prompt, jnp.arange(PROMPTS, dtype=jnp.int32))
```

```python
import functools

import jax
import jax.numpy as jnp
from jax import lax
from jax.experimental import pallas as pl
from jax.experimental.pallas import tpu as pltpu
from jax.sharding import Mesh
from jax.sharding import PartitionSpec as P

H = 32
KVH = 8
GRP = H // KVH
HD = 128
KW = KVH * HD
QW = H * HD
SCALE = HD**-0.5
LOG2E = 1.4426950408889634
EXP_SCALE = SCALE * LOG2E
STAT = 2 * HD

NT = (((1,), (1,)), ((), ()))
NN = (((1,), (0,)), ((), ()))


def dot(a, b, dims):
    return lax.dot_general(a, b, dims, preferred_element_type=jnp.float32)


def three_parts(x):
    hi = x.astype(jnp.bfloat16).astype(jnp.float32)
    rest = x - hi
    mid = rest.astype(jnp.bfloat16).astype(jnp.float32)
    low = rest - mid
    return (hi + pltpu.roll(mid, 32, 1) + pltpu.roll(low, 64, 1)).astype(jnp.bfloat16)


def from_parts(x):
    x = x.astype(jnp.float32)
    return (pltpu.roll(x, HD - 64, 1) + pltpu.roll(x, HD - 32, 1)) + x


def prefix_kernel(info, q_ref, own_ref, other_ref, out_ref, cache, sems):
    count = q_ref.shape[0]
    positions = cache.shape[0]
    active = info[0]
    length = info[2]

    def copies(src):
        return [
            pltpu.make_async_copy(
                src.at[:, pl.ds(k * 2 * HD, 2 * HD)],
                cache.at[:, pl.ds(k * 2 * HD, 2 * HD)],
                sems.at[k],
            )
            for k in range(KVH)
        ]

    order = [0, 4, 1, 5, 2, 6, 3, 7]

    @pl.when(active == 1)
    def _():
        cs = copies(own_ref)
        for k in order:
            cs[k].start()

    @pl.when(active == 2)
    def _():
        cs = copies(other_ref)
        for k in order:
            cs[k].start()

    @pl.when(active > 0)
    def _():
        waits = copies(own_ref)
        lane = lax.broadcasted_iota(jnp.int32, (count, HD), 1)
        pos = lax.broadcasted_iota(jnp.int32, (1, positions), 1)
        bias = jnp.where(pos < length, 0.0, -1e30).astype(jnp.float32)

        def head(g, stats):
            m_all, l_all = stats
            q = jnp.concatenate(
                [
                    q_ref[:, pl.ds(pl.multiple_of((g * GRP + j) * HD, HD), HD)]
                    for j in range(GRP)
                ],
                axis=0,
            )
            keys = cache[:, pl.ds(pl.multiple_of(g * HD, HD), HD)]
            values = cache[:, pl.ds(pl.multiple_of(KW + g * HD, HD), HD)]
            s = dot(q, keys, NT) + bias
            top = jnp.max(s, axis=1, keepdims=True)
            e = jnp.exp2((s - top) * EXP_SCALE)
            total = jnp.sum(e, axis=1, keepdims=True)
            o = dot(e.astype(jnp.bfloat16), values, NN)
            for j in range(GRP):
                rows = slice(j * count, (j + 1) * count)
                out_ref[:, pl.ds(pl.multiple_of((g * GRP + j) * HD, HD), HD)] = o[rows].astype(
                    out_ref.dtype
                )
                here = lane == g * GRP + j
                m_all = jnp.where(here, top[rows], m_all)
                l_all = jnp.where(here, total[rows], l_all)
            return m_all, l_all

        stats = (jnp.zeros((count, HD), jnp.float32), jnp.zeros((count, HD), jnp.float32))
        for pair in range(KVH // 2):
            waits[pair].wait()
            waits[pair + 4].wait()
            stats = lax.fori_loop(2 * pair, 2 * pair + 2, head, stats)
        out_ref[:, pl.ds(QW, HD)] = three_parts(stats[0])
        out_ref[:, pl.ds(QW + HD, HD)] = three_parts(stats[1])


def prefix_call(info, q, own, other):
    count = q.shape[0]
    positions = own.shape[0]
    return pl.pallas_call(
        prefix_kernel,
        out_shape=jax.ShapeDtypeStruct((count, QW + STAT), jnp.bfloat16),
        in_specs=[
            pl.BlockSpec(memory_space=pltpu.SMEM),
            pl.BlockSpec(memory_space=pltpu.VMEM),
            pl.BlockSpec(memory_space=pl.ANY),
            pl.BlockSpec(memory_space=pl.ANY),
        ],
        out_specs=pl.BlockSpec(memory_space=pltpu.VMEM),
        scratch_shapes=[
            pltpu.VMEM((positions, 2 * KW), jnp.bfloat16),
            pltpu.SemaphoreType.DMA((KVH,)),
        ],
        cost_estimate=pl.CostEstimate(
            flops=4 * count * H * positions * HD,
            bytes_accessed=4 * positions * KW,
            transcendentals=count * H * positions,
        ),
        name="prefix",
    )(info, q, own, other)


def suffix_kernel(lens, q_ref, kv_ref, new_ref, o_ref, m_ref, l_ref):
    step = pl.program_id(0)
    positions = kv_ref.shape[1]
    q = q_ref[0].astype(jnp.float32)
    group = lax.broadcasted_iota(jnp.int32, (H, HD), 0) // GRP
    spread = jnp.concatenate([jnp.where(group == g, q, 0.0) for g in range(KVH)], axis=1)
    new = new_ref[0].astype(jnp.float32)
    s = dot(spread.astype(jnp.bfloat16), kv_ref[0, :, :KW], NT)
    pos = lax.broadcasted_iota(jnp.int32, (1, positions), 1)
    s = jnp.where(pos < lens[step], s, -1e30)
    own = jnp.sum(spread * new[:, :KW], axis=1, keepdims=True)
    top = jnp.maximum(jnp.max(s, axis=1, keepdims=True), own)
    e = jnp.exp2((s - top) * EXP_SCALE)
    own_e = jnp.exp2((own - top) * EXP_SCALE)
    total = jnp.sum(e, axis=1, keepdims=True) + own_e
    o = dot(e.astype(jnp.bfloat16), kv_ref[0, :, KW:], NN)
    o = o + own_e.astype(jnp.bfloat16).astype(jnp.float32) * new[:, KW:]
    picked = o[:, :HD]
    for g in range(1, KVH):
        picked = jnp.where(group == g, o[:, g * HD : (g + 1) * HD], picked)
    top = jnp.broadcast_to(top, (H, HD))
    total = jnp.broadcast_to(total, (H, HD))
    here = lax.broadcasted_iota(jnp.int32, (o_ref.shape[0], HD), 0) == step
    for h in range(H):
        at = slice(h * HD, (h + 1) * HD)
        o_ref[:, at] = jnp.where(here, picked[h : h + 1], o_ref[:, at])
        m_ref[:, at] = jnp.where(here, top[h : h + 1], m_ref[:, at])
        l_ref[:, at] = jnp.where(here, total[h : h + 1], l_ref[:, at])


def suffix_call(lens, q, kv, new):
    count, positions = kv.shape[:2]
    whole = pl.BlockSpec((count, QW), lambda i, n: (0, 0))
    shape = jax.ShapeDtypeStruct((count, QW), jnp.float32)
    return pl.pallas_call(
        suffix_kernel,
        out_shape=(shape,) * 3,
        grid_spec=pltpu.PrefetchScalarGridSpec(
            num_scalar_prefetch=1,
            grid=(count,),
            in_specs=[
                pl.BlockSpec((1, H, HD), lambda i, n: (i, 0, 0)),
                pl.BlockSpec((1, positions, 2 * KW), lambda i, n: (i, 0, 0)),
                pl.BlockSpec((1, 1, 2 * KW), lambda i, n: (i, 0, 0)),
            ],
            out_specs=(whole,) * 3,
        ),
        compiler_params=pltpu.CompilerParams(dimension_semantics=("arbitrary",)),
        cost_estimate=pl.CostEstimate(
            flops=4 * count * H * positions * KW,
            bytes_accessed=4 * count * positions * KW,
            transcendentals=count * H * positions,
        ),
        name="suffix",
    )(lens, q, kv, new)


def combine_kernel(where, got_ref, o_ref, m_ref, l_ref, out_ref):
    src = where[0]
    m_pre = from_parts(got_ref[src, :, QW : QW + HD])
    l_pre = from_parts(got_ref[src, :, QW + HD :])
    count = m_pre.shape[0]
    for h in range(H):
        at = slice(h * HD, (h + 1) * HD)
        m_suf = m_ref[:, at]
        m_h = jnp.broadcast_to(m_pre[:, h : h + 1], (count, HD))
        l_h = jnp.broadcast_to(l_pre[:, h : h + 1], (count, HD))
        top = jnp.maximum(m_h, m_suf)
        f_pre = jnp.exp2((m_h - top) * EXP_SCALE)
        f_suf = jnp.exp2((m_suf - top) * EXP_SCALE)
        numer = got_ref[src, :, at].astype(jnp.float32) * f_pre + o_ref[:, at] * f_suf
        denom = l_h * f_pre + l_ref[:, at] * f_suf
        attn = (numer / denom).astype(jnp.bfloat16)
        for k in range(out_ref.shape[0]):
            out_ref[k, :, at] = attn


def combine_call(where, got, o, m, l):
    peers, count, _ = got.shape
    vmem = pl.BlockSpec(memory_space=pltpu.VMEM)
    return pl.pallas_call(
        combine_kernel,
        out_shape=jax.ShapeDtypeStruct((peers, count, QW), jnp.bfloat16),
        in_specs=[pl.BlockSpec(memory_space=pltpu.SMEM), vmem, vmem, vmem, vmem],
        out_specs=vmem,
        name="combine",
    )(where, got, o, m, l)


CHIP = ("x", "z")


def to_chips(x):
    return lax.all_to_all(x, CHIP, split_axis=0, concat_axis=0, tiled=True)


def partner(x):
    return lax.ppermute(x, "core", [(0, 1), (1, 0)])


def local(queries, prompt_cache, owner, prompt_len, suffix_cache, suffix_len, new_kv, out_weight):
    peers = lax.axis_size(CHIP)
    core = lax.axis_index("core")
    q = queries[0]
    count = q.shape[0]
    all_q = to_chips(jnp.broadcast_to(q, (peers, *q.shape))).reshape(peers * count, QW)
    own_cache = prompt_cache[0, 0]
    other_cache = partner(own_cache)
    other_weight = partner(out_weight)

    o_suf, m_suf, l_suf = suffix_call(
        suffix_len[0], q.reshape(count, H, HD), suffix_cache[0], new_kv[0][:, None, :]
    )

    chip = owner[0] // 2
    mine = lax.axis_index(CHIP) == chip
    active = jnp.where(mine, jnp.where(owner[0] % 2 == core, 1, 2), 0)
    info = jnp.stack([active, chip, prompt_len[0]]).astype(jnp.int32)
    sent = prefix_call(info, all_q, own_cache, other_cache)
    got = to_chips(sent.reshape(peers, count, QW + STAT))
    attn = combine_call(chip[None], got, o_suf, m_suf, l_suf)
    attn = to_chips(attn).reshape(peers * count, QW)

    theirs = jnp.dot(attn, other_weight, preferred_element_type=jnp.float32).astype(jnp.bfloat16)
    back = partner(theirs).reshape(peers, count, -1)
    ours = jnp.dot(attn, out_weight, preferred_element_type=jnp.float32).astype(jnp.bfloat16)
    ours = ours.reshape(peers, count, -1)
    first = core == 0
    mixed = jnp.stack([jnp.where(first, ours, back), jnp.where(first, back, ours)], axis=1)
    return mixed.reshape(1, 2 * peers * count, -1)


def solution(mesh):
    prompts = mesh.devices.shape[0]
    fine = Mesh(mesh.devices.reshape(prompts, 4, 2, 2), ("prompt", "x", "z", "core"))
    sample = ("x", "z", "core")
    in_specs = (
        P("prompt", sample, None),
        P("prompt", sample, None, None),
        P("prompt"),
        P("prompt"),
        P("prompt", sample, None, None),
        P("prompt", sample),
        P("prompt", sample, None),
        P(None, sample),
    )
    out_specs = P("prompt", None, sample)
    return jax.shard_map(local, mesh=fine, in_specs=in_specs, out_specs=out_specs, check_vma=False)
```

```python
import functools

import jax
import jax.numpy as jnp
from jax import lax
from jax.experimental import pallas as pl
from jax.experimental.pallas import tpu as pltpu
from jax.sharding import Mesh
from jax.sharding import PartitionSpec as P


H = 32
KVH = 8
GRP = H // KVH
HD = 128
KW = KVH * HD
QW = H * HD
SCALE = HD**-0.5
LOG2E = 1.4426950408889634
EXP_SCALE = SCALE * LOG2E
STAT = 2 * HD

NT = (((1,), (1,)), ((), ()))
NN = (((1,), (0,)), ((), ()))


def dot(a, b, dims):
    return lax.dot_general(a, b, dims, preferred_element_type=jnp.float32)


def three_parts(x):
    hi = x.astype(jnp.bfloat16).astype(jnp.float32)
    rest = x - hi
    mid = rest.astype(jnp.bfloat16).astype(jnp.float32)
    low = rest - mid
    return (hi + pltpu.roll(mid, 32, 1) + pltpu.roll(low, 64, 1)).astype(jnp.bfloat16)


def from_parts(x):
    x = x.astype(jnp.float32)
    return (pltpu.roll(x, HD - 64, 1) + pltpu.roll(x, HD - 32, 1)) + x


def prefix_kernel(info, q_ref, own_ref, other_ref, out_ref, cache, even, odd, sems):
    count = q_ref.shape[0]
    positions = cache.shape[0]
    active = info[0]
    length = info[2]
    pairs = KVH // 2

    def copies(src):
        cols = [pl.ds(k * 2 * HD, 2 * HD) for k in range(KVH)]
        return [
            pltpu.make_async_copy(src.at[:, at], cache.at[:, at], sems.at[k])
            for k, at in enumerate(cols)
        ]

    def start(src):
        cs = copies(src)
        for k in range(pairs):
            cs[k].start()
            cs[pairs + k].start()

    @pl.when(active == 1)
    def _():
        start(own_ref)

    @pl.when(active == 2)
    def _():
        start(other_ref)

    @pl.when(active > 0)
    def _():
        waits = copies(own_ref)
        lane = lax.broadcasted_iota(jnp.int32, (count, HD), 1)
        pos = lax.broadcasted_iota(jnp.int32, (1, positions), 1)
        bias = jnp.where(pos < length, 0.0, -1e30).astype(jnp.float32)
        first = lax.broadcasted_iota(jnp.int32, (positions, HD), 1) == 0
        ones = jnp.where(first, 1.0, 0.0).astype(jnp.bfloat16)
        held = (even, odd)

        def score(g):
            if g % 2 == 0:
                waits[g // 2].wait()
            if g % 2 == 0 and g:
                waits[pairs + g // 2].wait()
            q = [q_ref[:, h * HD : (h + 1) * HD] for h in range(g * GRP, (g + 1) * GRP)]
            s = dot(jnp.concatenate(q, axis=0), cache[:, g * HD : (g + 1) * HD], NT) + bias
            held[g % 2][...] = s
            return jnp.max(s, axis=1, keepdims=True)

        m_all = jnp.zeros((count, HD), jnp.float32)
        l_all = jnp.zeros((count, HD), jnp.float32)
        tops = [score(0)]
        waits[pairs].wait()
        for g in range(KVH):
            if g < KVH - 1:
                tops.append(score(g + 1))
            top = tops[g]
            e = jnp.exp2((held[g % 2][...] - top) * EXP_SCALE)
            values = cache[:, KW + g * HD : KW + (g + 1) * HD]
            o = dot(e.astype(jnp.bfloat16), jnp.concatenate([values, ones], axis=1), NN)
            for j in range(GRP):
                rows = slice(j * count, (j + 1) * count)
                h = g * GRP + j
                out_ref[:, h * HD : (h + 1) * HD] = o[rows, :HD].astype(out_ref.dtype)
                m_all = jnp.where(lane == h, top[rows], m_all)
                l_all = jnp.where(lane == h, o[rows, HD : HD + 1], l_all)
        out_ref[:, QW : QW + HD] = three_parts(m_all)
        out_ref[:, QW + HD :] = three_parts(l_all)


def prefix_call(info, q, own, other):
    count = q.shape[0]
    positions = own.shape[0]
    vmem = pl.BlockSpec(memory_space=pltpu.VMEM)
    raw = pl.BlockSpec(memory_space=pl.ANY)
    return pl.pallas_call(
        prefix_kernel,
        out_shape=jax.ShapeDtypeStruct((count, QW + STAT), jnp.bfloat16),
        in_specs=[pl.BlockSpec(memory_space=pltpu.SMEM), vmem, raw, raw],
        out_specs=vmem,
        scratch_shapes=[
            pltpu.VMEM((positions, 2 * KW), jnp.bfloat16),
            pltpu.VMEM((GRP * count, positions), jnp.float32),
            pltpu.VMEM((GRP * count, positions), jnp.float32),
            pltpu.SemaphoreType.DMA((KVH,)),
        ],
        compiler_params=pltpu.CompilerParams(vmem_limit_bytes=52 << 20),
        cost_estimate=pl.CostEstimate(
            flops=4 * count * H * positions * HD,
            bytes_accessed=4 * positions * KW,
            transcendentals=count * H * positions,
        ),
        name="prefix",
    )(info, q, own, other)


def suffix_kernel(base, lens, q_ref, new_ref, kv_ref, out_ref, kv, rows, sems):
    count, positions = kv.shape[:2]
    mine = range(base, base + count)
    copies = {
        i: pltpu.make_async_copy(kv_ref.at[i], kv.at[i - base], sems.at[i - base]) for i in mine
    }
    for i in mine:
        copies[i].start()
    q = q_ref[...].astype(jnp.float32)
    new = new_ref[...].astype(jnp.float32)
    group = lax.broadcasted_iota(jnp.int32, (H, HD), 0) // GRP
    pos = lax.broadcasted_iota(jnp.int32, (1, positions), 1)
    for i in mine:
        for h in range(H):
            rows[i - base, h : h + 1, :] = q[i : i + 1, h * HD : (h + 1) * HD]
    for i in mine:
        heads = rows[i - base]
        spread = jnp.concatenate([jnp.where(group == g, heads, 0.0) for g in range(KVH)], axis=1)
        own = jnp.sum(spread * new[i : i + 1, :KW], axis=1, keepdims=True)
        copies[i].wait()
        s = dot(spread.astype(jnp.bfloat16), kv[i - base, :, :KW], NT)
        s = jnp.where(pos < lens[i], s, -1e30)
        top = jnp.maximum(jnp.max(s, axis=1, keepdims=True), own)
        e = jnp.exp2((s - top) * EXP_SCALE)
        own_e = jnp.exp2((own - top) * EXP_SCALE)
        total = jnp.sum(e, axis=1, keepdims=True) + own_e
        o = dot(e.astype(jnp.bfloat16), kv[i - base, :, KW:], NN)
        o = o + own_e.astype(jnp.bfloat16).astype(jnp.float32) * new[i : i + 1, KW:]
        picked = o[:, :HD]
        for g in range(1, KVH):
            picked = jnp.where(group == g, o[:, g * HD : (g + 1) * HD], picked)
        top = jnp.broadcast_to(top, (H, HD))
        total = jnp.broadcast_to(total, (H, HD))
        for h in range(H):
            for k, part in enumerate((picked, top, total)):
                out_ref[i : i + 1, k * QW + h * HD : k * QW + (h + 1) * HD] = part[h : h + 1]


def suffix_call(base, count, limit, lens, q, new, kv):
    samples, positions, width = kv.shape
    vmem = pl.BlockSpec(memory_space=pltpu.VMEM)
    return pl.pallas_call(
        functools.partial(suffix_kernel, base),
        out_shape=jax.ShapeDtypeStruct((samples, 3 * QW), jnp.float32),
        in_specs=[
            pl.BlockSpec(memory_space=pltpu.SMEM),
            vmem,
            vmem,
            pl.BlockSpec(memory_space=pl.ANY),
        ],
        out_specs=vmem,
        scratch_shapes=[
            pltpu.VMEM((count, positions, width), kv.dtype),
            pltpu.VMEM((count, H, HD), jnp.float32),
            pltpu.SemaphoreType.DMA((count,)),
        ],
        compiler_params=pltpu.CompilerParams(vmem_limit_bytes=limit << 20),
        cost_estimate=pl.CostEstimate(
            flops=4 * count * H * positions * KW,
            bytes_accessed=4 * count * positions * KW,
            transcendentals=count * H * positions,
        ),
        name="suffix",
    )(lens, q, new, kv)


def copies_kernel(x_ref, out_ref, x, sem):
    pltpu.async_copy(x_ref, x, sem).wait()
    for k in range(out_ref.shape[0]):
        out_ref[k] = x[...]


def copies_call(x, peers):
    return pl.pallas_call(
        copies_kernel,
        out_shape=jax.ShapeDtypeStruct((peers, *x.shape), x.dtype),
        in_specs=[pl.BlockSpec(memory_space=pl.ANY)],
        out_specs=pl.BlockSpec(memory_space=pltpu.VMEM),
        scratch_shapes=[pltpu.VMEM(x.shape, x.dtype), pltpu.SemaphoreType.DMA],
        compiler_params=pltpu.CompilerParams(vmem_limit_bytes=4 << 20),
        name="copies",
    )(x)


def stage_kernel(x_ref, out_ref, sem):
    pltpu.async_copy(x_ref, out_ref, sem).wait()


def stage_call(x):
    return pl.pallas_call(
        stage_kernel,
        out_shape=jax.ShapeDtypeStruct(x.shape, x.dtype),
        in_specs=[pl.BlockSpec(memory_space=pl.ANY)],
        out_specs=pl.BlockSpec(memory_space=pltpu.VMEM),
        scratch_shapes=[pltpu.SemaphoreType.DMA],
        compiler_params=pltpu.CompilerParams(vmem_limit_bytes=4 << 20),
        cost_estimate=pl.CostEstimate(flops=0, bytes_accessed=2 * x.size, transcendentals=0),
        name="stage",
    )(x)


def combine_kernel(split, where, got_ref, early, late, out_ref, attn, outs):
    src = where[0]
    m_pre = from_parts(got_ref[src, :, QW : QW + HD])
    l_pre = from_parts(got_ref[src, :, QW + HD :])
    count = m_pre.shape[0]
    first = lax.broadcasted_iota(jnp.int32, (count, HD), 0) < split
    for h in range(H):
        at = slice(h * HD, (h + 1) * HD)
        cols = [slice(k * QW + h * HD, k * QW + (h + 1) * HD) for k in range(3)]
        o_suf, m_suf, l_suf = (jnp.where(first, early[:, c], late[:, c]) for c in cols)
        m_h = jnp.broadcast_to(m_pre[:, h : h + 1], (count, HD))
        l_h = jnp.broadcast_to(l_pre[:, h : h + 1], (count, HD))
        top = jnp.maximum(m_h, m_suf)
        f_pre = jnp.exp2((m_h - top) * EXP_SCALE)
        f_suf = jnp.exp2((m_suf - top) * EXP_SCALE)
        numer = got_ref[src, :, at].astype(jnp.float32) * f_pre + o_suf * f_suf
        denom = l_h * f_pre + l_suf * f_suf
        attn[:, at] = (numer / denom).astype(jnp.bfloat16)
    copies = [pltpu.make_async_copy(attn, out_ref.at[k], outs.at[k]) for k in range(out_ref.shape[0])]
    for c in copies:
        c.start()
    for c in copies:
        c.wait()


def combine_call(split, where, got, early, late):
    peers, count, _ = got.shape
    vmem = pl.BlockSpec(memory_space=pltpu.VMEM)
    return pl.pallas_call(
        functools.partial(combine_kernel, split),
        out_shape=jax.ShapeDtypeStruct((peers, count, QW), jnp.bfloat16),
        in_specs=[pl.BlockSpec(memory_space=pltpu.SMEM), vmem, vmem, vmem],
        out_specs=pl.BlockSpec(memory_space=pl.ANY),
        scratch_shapes=[pltpu.VMEM((count, QW), jnp.bfloat16), pltpu.SemaphoreType.DMA((peers,))],
        compiler_params=pltpu.CompilerParams(vmem_limit_bytes=8 << 20),
        name="combine",
    )(where, got, early, late)


def project(x, w):
    return jnp.dot(x, w, preferred_element_type=jnp.float32).astype(jnp.bfloat16)


def join_kernel(info, ours_ref, back_ref, out_ref):
    count = ours_ref.shape[1]
    ours, back = ours_ref[...], back_ref[...]
    first = info[0] == 0
    out_ref[:, :count] = jnp.where(first, ours, back)
    out_ref[:, count:] = jnp.where(first, back, ours)


def join_call(core, ours, back):
    peers, count, cols = ours.shape
    vmem = pl.BlockSpec(memory_space=pltpu.VMEM)
    return pl.pallas_call(
        join_kernel,
        out_shape=jax.ShapeDtypeStruct((peers, 2 * count, cols), ours.dtype),
        in_specs=[pl.BlockSpec(memory_space=pltpu.SMEM), vmem, vmem],
        out_specs=vmem,
        compiler_params=pltpu.CompilerParams(vmem_limit_bytes=4 << 20),
        name="join",
    )(core, ours, back)


CHIP = ("x", "z")


def to_chips(x):
    return lax.all_to_all(x, CHIP, split_axis=0, concat_axis=0, tiled=True)


def partner(x):
    return lax.ppermute(x, "core", [(0, 1), (1, 0)])


def local(queries, prompt_cache, owner, prompt_len, suffix_cache, suffix_len, new_kv, out_weight):
    peers = lax.axis_size(CHIP)
    core = lax.axis_index("core")
    q = queries[0]
    count = q.shape[0]
    split = 5
    own_cache = prompt_cache[0, 0]
    chip = owner[0] // 2
    mine = lax.axis_index(CHIP) == chip
    active = jnp.where(mine, jnp.where(owner[0] % 2 == core, 1, 2), 0)
    info = jnp.stack([active, chip, prompt_len[0]]).astype(jnp.int32)
    suffix_args = (suffix_len[0], q, new_kv[0], suffix_cache[0])
    other_cache = partner(own_cache)
    all_q = to_chips(copies_call(q, peers)).reshape(peers * count, QW)
    early = suffix_call(0, split, 57, *suffix_args)
    sent = prefix_call(info, all_q, own_cache, other_cache)
    got = to_chips(sent.reshape(peers, count, QW + STAT))
    late = suffix_call(split, count - split, 50, *suffix_args)
    attn = combine_call(split, chip[None], got, early, late)
    attn = to_chips(attn).reshape(peers * count, QW)
    other_weight = partner(out_weight)
    other_weight = stage_call(other_weight)
    theirs = project(attn, other_weight)
    back = partner(theirs).reshape(peers, count, -1)
    ours = project(attn, out_weight).reshape(peers, count, -1)
    mixed = join_call(core[None], ours, back)
    return mixed.reshape(1, 2 * peers * count, -1)


def solution(mesh):
    prompts = mesh.devices.shape[0]
    fine = Mesh(mesh.devices.reshape(prompts, 4, 2, 2), ("prompt", "x", "z", "core"))
    sample = ("x", "z", "core")
    in_specs = (
        P("prompt", sample, None),
        P("prompt", sample, None, None),
        P("prompt"),
        P("prompt"),
        P("prompt", sample, None, None),
        P("prompt", sample),
        P("prompt", sample, None),
        P(None, sample),
    )
    out_specs = P("prompt", None, sample)
    return jax.shard_map(local, mesh=fine, in_specs=in_specs, out_specs=out_specs, check_vma=False)
```

```python
import functools

import jax
import jax.numpy as jnp
from jax import lax
from jax.experimental import pallas as pl
from jax.experimental.pallas import tpu as pltpu
from jax.sharding import Mesh
from jax.sharding import PartitionSpec as P


H = 32
KVH = 8
GRP = H // KVH
HD = 128
KW = KVH * HD
QW = H * HD
SCALE = HD**-0.5
LOG2E = 1.4426950408889634
EXP_SCALE = SCALE * LOG2E
GROUPS = (1, 3, 8)
STAT = 2 * HD

NT = (((1,), (1,)), ((), ()))
NN = (((1,), (0,)), ((), ()))


def dot(a, b, dims):
    return lax.dot_general(a, b, dims, preferred_element_type=jnp.float32)


def three_parts(x):
    hi = x.astype(jnp.bfloat16).astype(jnp.float32)
    rest = x - hi
    mid = rest.astype(jnp.bfloat16).astype(jnp.float32)
    low = rest - mid
    return (hi + pltpu.roll(mid, 32, 1) + pltpu.roll(low, 64, 1)).astype(jnp.bfloat16)


def from_parts(x):
    x = x.astype(jnp.float32)
    return (pltpu.roll(x, HD - 64, 1) + pltpu.roll(x, HD - 32, 1)) + x


def prefix_kernel(info, q_ref, own_ref, other_ref, out_ref, cache, even, odd, sems):
    count = q_ref.shape[0]
    positions = cache.shape[0]
    active = info[0]
    length = info[2]
    ends = GROUPS

    def copies(src):
        found = []
        for k, (lo, hi) in enumerate(zip((0, *ends[:-1]), ends)):
            for part in range(2):
                at = pl.ds(part * KW + lo * HD, (hi - lo) * HD)
                sem = sems.at[2 * k + part]
                found.append(pltpu.make_async_copy(src.at[:, at], cache.at[:, at], sem))
        return found

    def start(src):
        for c in copies(src):
            c.start()

    @pl.when(active == 1)
    def _():
        start(own_ref)

    @pl.when(active == 2)
    def _():
        start(other_ref)

    @pl.when(active > 0)
    def _():
        waits = copies(own_ref)
        lane = lax.broadcasted_iota(jnp.int32, (count, HD), 1)
        pos = lax.broadcasted_iota(jnp.int32, (1, positions), 1)
        bias = jnp.where(pos < length, 0.0, -1e30).astype(jnp.float32)
        first = lax.broadcasted_iota(jnp.int32, (positions, HD), 1) == 0
        ones = jnp.where(first, 1.0, 0.0).astype(jnp.bfloat16)
        held = (even, odd)

        def score(g):
            if g == 0 or g in ends:
                k = 0 if g == 0 else ends.index(g) + 1
                waits[2 * k].wait()
                waits[2 * k + 1].wait()
            q = [q_ref[:, h * HD : (h + 1) * HD] for h in range(g * GRP, (g + 1) * GRP)]
            s = dot(jnp.concatenate(q, axis=0), cache[:, g * HD : (g + 1) * HD], NT) + bias
            held[g % 2][...] = s
            return jnp.max(s, axis=1, keepdims=True)

        m_all = jnp.zeros((count, HD), jnp.float32)
        l_all = jnp.zeros((count, HD), jnp.float32)
        tops = [score(0)]
        for g in range(KVH):
            if g < KVH - 1:
                tops.append(score(g + 1))
            top = tops[g]
            e = jnp.exp2((held[g % 2][...] - top) * EXP_SCALE)
            values = cache[:, KW + g * HD : KW + (g + 1) * HD]
            o = dot(e.astype(jnp.bfloat16), jnp.concatenate([values, ones], axis=1), NN)
            for j in range(GRP):
                rows = slice(j * count, (j + 1) * count)
                h = g * GRP + j
                out_ref[:, h * HD : (h + 1) * HD] = o[rows, :HD].astype(out_ref.dtype)
                m_all = jnp.where(lane == h, top[rows], m_all)
                l_all = jnp.where(lane == h, o[rows, HD : HD + 1], l_all)
        out_ref[:, QW : QW + HD] = three_parts(m_all)
        out_ref[:, QW + HD :] = three_parts(l_all)


def prefix_call(info, q, own, other):
    count = q.shape[0]
    positions = own.shape[0]
    vmem = pl.BlockSpec(memory_space=pltpu.VMEM)
    raw = pl.BlockSpec(memory_space=pl.ANY)
    return pl.pallas_call(
        prefix_kernel,
        out_shape=jax.ShapeDtypeStruct((count, QW + STAT), jnp.bfloat16),
        in_specs=[pl.BlockSpec(memory_space=pltpu.SMEM), vmem, raw, raw],
        out_specs=vmem,
        scratch_shapes=[
            pltpu.VMEM((positions, 2 * KW), jnp.bfloat16),
            pltpu.VMEM((GRP * count, positions), jnp.float32),
            pltpu.VMEM((GRP * count, positions), jnp.float32),
            pltpu.SemaphoreType.DMA((2 * len(GROUPS),)),
        ],
        compiler_params=pltpu.CompilerParams(vmem_limit_bytes=52 << 20),
        cost_estimate=pl.CostEstimate(
            flops=4 * count * H * positions * HD,
            bytes_accessed=4 * positions * KW,
            transcendentals=count * H * positions,
        ),
        name="prefix",
    )(info, q, own, other)


def suffix_kernel(base, lens, q_ref, new_ref, kv_ref, out_ref, kv, rows, sems):
    count, positions = kv.shape[:2]
    mine = range(base, base + count)
    copies = {
        i: pltpu.make_async_copy(kv_ref.at[i], kv.at[i - base], sems.at[i - base]) for i in mine
    }
    for i in mine:
        copies[i].start()
    q = q_ref[...].astype(jnp.float32)
    new = new_ref[...].astype(jnp.float32)
    group = lax.broadcasted_iota(jnp.int32, (H, HD), 0) // GRP
    pos = lax.broadcasted_iota(jnp.int32, (1, positions), 1)
    for i in mine:
        for h in range(H):
            rows[i - base, h : h + 1, :] = q[i : i + 1, h * HD : (h + 1) * HD]
    for i in mine:
        heads = rows[i - base]
        spread = jnp.concatenate([jnp.where(group == g, heads, 0.0) for g in range(KVH)], axis=1)
        own = jnp.sum(spread * new[i : i + 1, :KW], axis=1, keepdims=True)
        copies[i].wait()
        s = dot(spread.astype(jnp.bfloat16), kv[i - base, :, :KW], NT)
        s = jnp.where(pos < lens[i], s, -1e30)
        top = jnp.maximum(jnp.max(s, axis=1, keepdims=True), own)
        e = jnp.exp2((s - top) * EXP_SCALE)
        own_e = jnp.exp2((own - top) * EXP_SCALE)
        total = jnp.sum(e, axis=1, keepdims=True) + own_e
        o = dot(e.astype(jnp.bfloat16), kv[i - base, :, KW:], NN)
        o = o + own_e.astype(jnp.bfloat16).astype(jnp.float32) * new[i : i + 1, KW:]
        picked = o[:, :HD]
        for g in range(1, KVH):
            picked = jnp.where(group == g, o[:, g * HD : (g + 1) * HD], picked)
        top = jnp.broadcast_to(top, (H, HD))
        total = jnp.broadcast_to(total, (H, HD))
        for h in range(H):
            for k, part in enumerate((picked, top, total)):
                out_ref[i : i + 1, k * QW + h * HD : k * QW + (h + 1) * HD] = part[h : h + 1]


def suffix_call(base, count, limit, lens, q, new, kv):
    samples, positions, width = kv.shape
    vmem = pl.BlockSpec(memory_space=pltpu.VMEM)
    return pl.pallas_call(
        functools.partial(suffix_kernel, base),
        out_shape=jax.ShapeDtypeStruct((samples, 3 * QW), jnp.float32),
        in_specs=[
            pl.BlockSpec(memory_space=pltpu.SMEM),
            vmem,
            vmem,
            pl.BlockSpec(memory_space=pl.ANY),
        ],
        out_specs=vmem,
        scratch_shapes=[
            pltpu.VMEM((count, positions, width), kv.dtype),
            pltpu.VMEM((count, H, HD), jnp.float32),
            pltpu.SemaphoreType.DMA((count,)),
        ],
        compiler_params=pltpu.CompilerParams(vmem_limit_bytes=limit << 20),
        cost_estimate=pl.CostEstimate(
            flops=4 * count * H * positions * KW,
            bytes_accessed=4 * count * positions * KW,
            transcendentals=count * H * positions,
        ),
        name="suffix",
    )(lens, q, new, kv)


def stage_kernel(x_ref, out_ref, sem):
    pltpu.async_copy(x_ref, out_ref, sem).wait()


def stage_call(x):
    return pl.pallas_call(
        stage_kernel,
        out_shape=jax.ShapeDtypeStruct(x.shape, x.dtype),
        in_specs=[pl.BlockSpec(memory_space=pl.ANY)],
        out_specs=pl.BlockSpec(memory_space=pltpu.VMEM),
        scratch_shapes=[pltpu.SemaphoreType.DMA],
        compiler_params=pltpu.CompilerParams(vmem_limit_bytes=4 << 20),
        cost_estimate=pl.CostEstimate(flops=0, bytes_accessed=2 * x.size, transcendentals=0),
        name="stage",
    )(x)


def combine_kernel(split, where, got_ref, early, late, out_ref, attn, outs):
    src = where[0]
    m_pre = from_parts(got_ref[src, :, QW : QW + HD])
    l_pre = from_parts(got_ref[src, :, QW + HD :])
    count = m_pre.shape[0]
    first = lax.broadcasted_iota(jnp.int32, (count, HD), 0) < split
    for h in range(H):
        at = slice(h * HD, (h + 1) * HD)
        cols = [slice(k * QW + h * HD, k * QW + (h + 1) * HD) for k in range(3)]
        o_suf, m_suf, l_suf = (jnp.where(first, early[:, c], late[:, c]) for c in cols)
        m_h = jnp.broadcast_to(m_pre[:, h : h + 1], (count, HD))
        l_h = jnp.broadcast_to(l_pre[:, h : h + 1], (count, HD))
        top = jnp.maximum(m_h, m_suf)
        f_pre = jnp.exp2((m_h - top) * EXP_SCALE)
        f_suf = jnp.exp2((m_suf - top) * EXP_SCALE)
        numer = got_ref[src, :, at].astype(jnp.float32) * f_pre + o_suf * f_suf
        denom = l_h * f_pre + l_suf * f_suf
        attn[:, at] = (numer / denom).astype(jnp.bfloat16)
    copies = [pltpu.make_async_copy(attn, out_ref.at[k], outs.at[k]) for k in range(out_ref.shape[0])]
    for c in copies:
        c.start()
    for c in copies:
        c.wait()


def combine_call(split, where, got, early, late):
    peers, count, _ = got.shape
    vmem = pl.BlockSpec(memory_space=pltpu.VMEM)
    return pl.pallas_call(
        functools.partial(combine_kernel, split),
        out_shape=jax.ShapeDtypeStruct((peers, count, QW), jnp.bfloat16),
        in_specs=[pl.BlockSpec(memory_space=pltpu.SMEM), vmem, vmem, vmem],
        out_specs=pl.BlockSpec(memory_space=pl.ANY),
        scratch_shapes=[pltpu.VMEM((count, QW), jnp.bfloat16), pltpu.SemaphoreType.DMA((peers,))],
        compiler_params=pltpu.CompilerParams(vmem_limit_bytes=8 << 20),
        name="combine",
    )(where, got, early, late)


def project(x, w):
    return jnp.dot(x, w, preferred_element_type=jnp.float32).astype(jnp.bfloat16)


def join_kernel(info, ours_ref, back_ref, out_ref):
    count = ours_ref.shape[1]
    ours, back = ours_ref[...], back_ref[...]
    first = info[0] == 0
    out_ref[:, :count] = jnp.where(first, ours, back)
    out_ref[:, count:] = jnp.where(first, back, ours)


def join_call(core, ours, back):
    peers, count, cols = ours.shape
    vmem = pl.BlockSpec(memory_space=pltpu.VMEM)
    return pl.pallas_call(
        join_kernel,
        out_shape=jax.ShapeDtypeStruct((peers, 2 * count, cols), ours.dtype),
        in_specs=[pl.BlockSpec(memory_space=pltpu.SMEM), vmem, vmem],
        out_specs=vmem,
        compiler_params=pltpu.CompilerParams(vmem_limit_bytes=4 << 20),
        name="join",
    )(core, ours, back)


CHIP = ("x", "z")


def to_chips(x):
    return lax.all_to_all(x, CHIP, split_axis=0, concat_axis=0, tiled=True)


def partner(x):
    return lax.ppermute(x, "core", [(0, 1), (1, 0)])


def local(queries, prompt_cache, owner, prompt_len, suffix_cache, suffix_len, new_kv, out_weight):
    peers = lax.axis_size(CHIP)
    core = lax.axis_index("core")
    q = queries[0]
    count = q.shape[0]
    split = 4
    own_cache = prompt_cache[0, 0]
    chip = owner[0] // 2
    mine = lax.axis_index(CHIP) == chip
    active = jnp.where(mine, jnp.where(owner[0] % 2 == core, 1, 2), 0)
    info = jnp.stack([active, chip, prompt_len[0]]).astype(jnp.int32)
    suffix_args = (suffix_len[0], q, new_kv[0], suffix_cache[0])
    other_cache = partner(own_cache)
    q_copies = jnp.broadcast_to(q, (peers, *q.shape))
    all_q = to_chips(q_copies).reshape(peers * count, QW)
    early = suffix_call(0, split, 57, *suffix_args)
    sent = prefix_call(info, all_q, own_cache, other_cache)
    got = to_chips(sent.reshape(peers, count, QW + STAT))
    late = suffix_call(split, count - split, 50, *suffix_args)
    attn = combine_call(split, chip[None], got, early, late)
    attn = to_chips(attn).reshape(peers * count, QW)
    other_weight = partner(out_weight)
    other_weight = stage_call(other_weight)
    theirs = project(attn, other_weight)
    back = partner(theirs).reshape(peers, count, -1)
    ours = project(attn, out_weight).reshape(peers, count, -1)
    mixed = join_call(core[None], ours, back)
    return mixed.reshape(1, 2 * peers * count, -1)


def solution(mesh):
    prompts = mesh.devices.shape[0]
    fine = Mesh(mesh.devices.reshape(prompts, 4, 2, 2), ("prompt", "x", "z", "core"))
    sample = ("x", "z", "core")
    in_specs = (
        P("prompt", sample, None),
        P("prompt", sample, None, None),
        P("prompt"),
        P("prompt"),
        P("prompt", sample, None, None),
        P("prompt", sample),
        P("prompt", sample, None),
        P(None, sample),
    )
    out_specs = P("prompt", None, sample)
    return jax.shard_map(local, mesh=fine, in_specs=in_specs, out_specs=out_specs, check_vma=False)
```

```python
import jax
import jax.numpy as jnp
from jax import lax
from jax.experimental import pallas as pl
from jax.experimental.pallas import tpu as pltpu
from jax.sharding import Mesh
from jax.sharding import PartitionSpec as P


H = 32
KVH = 8
GRP = H // KVH
HD = 128
KW = KVH * HD
QW = H * HD
SCALE = HD**-0.5
LOG2E = 1.4426950408889634
EXP_SCALE = SCALE * LOG2E
GROUPS = (1, 3, 8)
CHIP = ("x", "z")
STAT = 2 * HD

NT = (((1,), (1,)), ((), ()))
NN = (((1,), (0,)), ((), ()))


def dot(a, b, dims):
    return lax.dot_general(a, b, dims, preferred_element_type=jnp.float32)


def three_parts(x):
    hi = x.astype(jnp.bfloat16).astype(jnp.float32)
    rest = x - hi
    mid = rest.astype(jnp.bfloat16).astype(jnp.float32)
    low = rest - mid
    return (hi + pltpu.roll(mid, 32, 1) + pltpu.roll(low, 64, 1)).astype(jnp.bfloat16)


def from_parts(x):
    x = x.astype(jnp.float32)
    return (pltpu.roll(x, HD - 64, 1) + pltpu.roll(x, HD - 32, 1)) + x


def prefix_kernel(owner, lens, q_ref, own_ref, other_ref, out_ref, cache, even, odd, sems):
    count = q_ref.shape[0]
    positions = cache.shape[0]
    here = lax.axis_index(CHIP) == lax.div(owner[0], 2)
    same = lax.axis_index("core") == lax.rem(owner[0], 2)
    length = lens[0]
    ends = GROUPS

    def copies(src):
        found = []
        for k, (lo, hi) in enumerate(zip((0, *ends[:-1]), ends)):
            for part in range(2):
                at = pl.ds(part * KW + lo * HD, (hi - lo) * HD)
                sem = sems.at[2 * k + part]
                found.append(pltpu.make_async_copy(src.at[:, at], cache.at[:, at], sem))
        return found

    def start(src):
        for c in copies(src):
            c.start()

    @pl.when(here & same)
    def _():
        start(own_ref)

    @pl.when(here & jnp.logical_not(same))
    def _():
        start(other_ref)

    @pl.when(here)
    def _():
        waits = copies(own_ref)
        lane = lax.broadcasted_iota(jnp.int32, (count, HD), 1)
        pos = lax.broadcasted_iota(jnp.int32, (1, positions), 1)
        bias = jnp.where(pos < length, 0.0, -1e30).astype(jnp.float32)
        first = lax.broadcasted_iota(jnp.int32, (positions, HD), 1) == 0
        ones = jnp.where(first, 1.0, 0.0).astype(jnp.bfloat16)
        held = (even, odd)

        def score(g):
            if g == 0 or g in ends:
                k = 0 if g == 0 else ends.index(g) + 1
                waits[2 * k].wait()
                waits[2 * k + 1].wait()
            q = [q_ref[:, h * HD : (h + 1) * HD] for h in range(g * GRP, (g + 1) * GRP)]
            s = dot(jnp.concatenate(q, axis=0), cache[:, g * HD : (g + 1) * HD], NT) + bias
            held[g % 2][...] = s
            return jnp.max(s, axis=1, keepdims=True)

        m_all = jnp.zeros((count, HD), jnp.float32)
        l_all = jnp.zeros((count, HD), jnp.float32)
        tops = [score(0)]
        for g in range(KVH):
            if g < KVH - 1:
                tops.append(score(g + 1))
            top = tops[g]
            e = jnp.exp2((held[g % 2][...] - top) * EXP_SCALE)
            values = cache[:, KW + g * HD : KW + (g + 1) * HD]
            o = dot(e.astype(jnp.bfloat16), jnp.concatenate([values, ones], axis=1), NN)
            for j in range(GRP):
                rows = slice(j * count, (j + 1) * count)
                h = g * GRP + j
                out_ref[:, h * HD : (h + 1) * HD] = o[rows, :HD].astype(out_ref.dtype)
                m_all = jnp.where(lane == h, top[rows], m_all)
                l_all = jnp.where(lane == h, o[rows, HD : HD + 1], l_all)
        out_ref[:, QW : QW + HD] = three_parts(m_all)
        out_ref[:, QW + HD :] = three_parts(l_all)


def prefix_call(owner, lens, q, own, other):
    count = q.shape[0]
    positions = own.shape[0]
    vmem = pl.BlockSpec(memory_space=pltpu.VMEM)
    raw = pl.BlockSpec(memory_space=pl.ANY)
    smem = pl.BlockSpec(memory_space=pltpu.SMEM)
    return pl.pallas_call(
        prefix_kernel,
        out_shape=jax.ShapeDtypeStruct((count, QW + STAT), jnp.bfloat16),
        in_specs=[smem, smem, vmem, raw, raw],
        out_specs=vmem,
        scratch_shapes=[
            pltpu.VMEM((positions, 2 * KW), jnp.bfloat16),
            pltpu.VMEM((GRP * count, positions), jnp.float32),
            pltpu.VMEM((GRP * count, positions), jnp.float32),
            pltpu.SemaphoreType.DMA((2 * len(GROUPS),)),
        ],
        compiler_params=pltpu.CompilerParams(vmem_limit_bytes=52 << 20),
        cost_estimate=pl.CostEstimate(
            flops=4 * count * H * positions * HD,
            bytes_accessed=4 * positions * KW,
            transcendentals=count * H * positions,
        ),
        name="prefix",
    )(owner, lens, q, own, other)


def suffix_kernel(lens, q_ref, new_ref, kv_ref, out_ref, kv, rows, sems):
    count, positions = kv.shape[:2]
    copies = [pltpu.make_async_copy(kv_ref.at[i], kv.at[i], sems.at[i]) for i in range(count)]
    for c in copies:
        c.start()
    q = q_ref[...].astype(jnp.float32)
    new = new_ref[...].astype(jnp.float32)
    group = lax.broadcasted_iota(jnp.int32, (H, HD), 0) // GRP
    pos = lax.broadcasted_iota(jnp.int32, (1, positions), 1)
    for i in range(count):
        for h in range(H):
            rows[i, h : h + 1, :] = q[i : i + 1, h * HD : (h + 1) * HD]
    for i in range(count):
        heads = rows[i]
        spread = jnp.concatenate([jnp.where(group == g, heads, 0.0) for g in range(KVH)], axis=1)
        own = jnp.sum(spread * new[i : i + 1, :KW], axis=1, keepdims=True)
        copies[i].wait()
        s = dot(spread.astype(jnp.bfloat16), kv[i, :, :KW], NT)
        s = jnp.where(pos < lens[i], s, -1e30)
        top = jnp.maximum(jnp.max(s, axis=1, keepdims=True), own)
        e = jnp.exp2((s - top) * EXP_SCALE)
        own_e = jnp.exp2((own - top) * EXP_SCALE)
        total = jnp.sum(e, axis=1, keepdims=True) + own_e
        o = dot(e.astype(jnp.bfloat16), kv[i, :, KW:], NN)
        o = o + own_e.astype(jnp.bfloat16).astype(jnp.float32) * new[i : i + 1, KW:]
        picked = o[:, :HD]
        for g in range(1, KVH):
            picked = jnp.where(group == g, o[:, g * HD : (g + 1) * HD], picked)
        top = jnp.broadcast_to(top, (H, HD))
        total = jnp.broadcast_to(total, (H, HD))
        for h in range(H):
            for k, part in enumerate((picked, top, total)):
                out_ref[i : i + 1, k * QW + h * HD : k * QW + (h + 1) * HD] = part[h : h + 1]


def suffix_call(lens, q, new, kv):
    count, positions, width = kv.shape
    vmem = pl.BlockSpec(memory_space=pltpu.VMEM)
    return pl.pallas_call(
        suffix_kernel,
        out_shape=jax.ShapeDtypeStruct((count, 3 * QW), jnp.float32),
        in_specs=[
            pl.BlockSpec(memory_space=pltpu.SMEM),
            vmem,
            vmem,
            pl.BlockSpec(memory_space=pl.ANY),
        ],
        out_specs=vmem,
        scratch_shapes=[
            pltpu.VMEM((count, positions, width), kv.dtype),
            pltpu.VMEM((count, H, HD), jnp.float32),
            pltpu.SemaphoreType.DMA((count,)),
        ],
        compiler_params=pltpu.CompilerParams(vmem_limit_bytes=57 << 20),
        cost_estimate=pl.CostEstimate(
            flops=4 * count * H * positions * KW,
            bytes_accessed=4 * count * positions * KW,
            transcendentals=count * H * positions,
        ),
        name="suffix",
    )(lens, q, new, kv)


def combine_kernel(owner, got_ref, suf_ref, w_ref, out_ref, w_out, attn, outs, w_sem):
    load = pltpu.make_async_copy(w_ref, w_out, w_sem)
    load.start()
    src = lax.div(owner[0], 2)
    m_pre = from_parts(got_ref[src, :, QW : QW + HD])
    l_pre = from_parts(got_ref[src, :, QW + HD :])
    count = m_pre.shape[0]
    for h in range(H):
        at = slice(h * HD, (h + 1) * HD)
        cols = [slice(k * QW + h * HD, k * QW + (h + 1) * HD) for k in range(3)]
        o_suf, m_suf, l_suf = (suf_ref[:, c] for c in cols)
        m_h = jnp.broadcast_to(m_pre[:, h : h + 1], (count, HD))
        l_h = jnp.broadcast_to(l_pre[:, h : h + 1], (count, HD))
        top = jnp.maximum(m_h, m_suf)
        f_pre = jnp.exp2((m_h - top) * EXP_SCALE)
        f_suf = jnp.exp2((m_suf - top) * EXP_SCALE)
        numer = got_ref[src, :, at].astype(jnp.float32) * f_pre + o_suf * f_suf
        denom = l_h * f_pre + l_suf * f_suf
        attn[:, at] = (numer / denom).astype(jnp.bfloat16)
    copies = [pltpu.make_async_copy(attn, out_ref.at[k], outs.at[k]) for k in range(out_ref.shape[0])]
    for c in copies:
        c.start()
    for c in copies:
        c.wait()
    load.wait()


def combine_call(owner, got, suf, w):
    peers, count, _ = got.shape
    vmem = pl.BlockSpec(memory_space=pltpu.VMEM)
    raw = pl.BlockSpec(memory_space=pl.ANY)
    return pl.pallas_call(
        combine_kernel,
        out_shape=[
            jax.ShapeDtypeStruct((peers, count, QW), jnp.bfloat16),
            jax.ShapeDtypeStruct(w.shape, w.dtype),
        ],
        in_specs=[pl.BlockSpec(memory_space=pltpu.SMEM), vmem, vmem, raw],
        out_specs=[raw, vmem],
        scratch_shapes=[
            pltpu.VMEM((count, QW), jnp.bfloat16),
            pltpu.SemaphoreType.DMA((peers,)),
            pltpu.SemaphoreType.DMA,
        ],
        compiler_params=pltpu.CompilerParams(vmem_limit_bytes=8 << 20),
        name="combine",
    )(owner, got, suf, w)


def project(x, w):
    return jnp.dot(x, w, preferred_element_type=jnp.float32).astype(jnp.bfloat16)


def join_kernel(ours_ref, back_ref, out_ref):
    count = ours_ref.shape[1]
    ours, back = ours_ref[...], back_ref[...]
    first = lax.axis_index("core") == 0
    out_ref[:, :count] = jnp.where(first, ours, back)
    out_ref[:, count:] = jnp.where(first, back, ours)


def join_call(ours, back):
    peers, count, cols = ours.shape
    vmem = pl.BlockSpec(memory_space=pltpu.VMEM)
    return pl.pallas_call(
        join_kernel,
        out_shape=jax.ShapeDtypeStruct((peers, 2 * count, cols), ours.dtype),
        in_specs=[vmem, vmem],
        out_specs=vmem,
        compiler_params=pltpu.CompilerParams(vmem_limit_bytes=4 << 20),
        name="join",
    )(ours, back)


def to_chips(x):
    return lax.all_to_all(x, CHIP, split_axis=0, concat_axis=0, tiled=True)


def partner(x):
    return lax.ppermute(x, "core", [(0, 1), (1, 0)])


def local(queries, prompt_cache, owner, prompt_len, suffix_cache, suffix_len, new_kv, out_weight):
    peers = lax.axis_size(CHIP)
    q = queries[0]
    count = q.shape[0]
    own_cache = prompt_cache[0, 0]
    other_cache = partner(own_cache)
    all_q = to_chips(jnp.broadcast_to(q, (peers, *q.shape))).reshape(peers * count, QW)
    sent = prefix_call(owner, prompt_len, all_q, own_cache, other_cache)
    got = to_chips(sent.reshape(peers, count, QW + STAT))
    suf = suffix_call(suffix_len[0], q, new_kv[0], suffix_cache[0])
    other_weight = partner(out_weight)
    attn, other_weight = combine_call(owner, got, suf, other_weight)
    attn = to_chips(attn).reshape(peers * count, QW)
    theirs = project(attn, other_weight)
    back = partner(theirs).reshape(peers, count, -1)
    ours = project(attn, out_weight).reshape(peers, count, -1)
    mixed = join_call(ours, back)
    return mixed.reshape(1, 2 * peers * count, -1)


def solution(mesh):
    prompts = mesh.devices.shape[0]
    fine = Mesh(mesh.devices.reshape(prompts, 4, 2, 2), ("prompt", "x", "z", "core"))
    sample = ("x", "z", "core")
    in_specs = (
        P("prompt", sample, None),
        P("prompt", sample, None, None),
        P("prompt"),
        P("prompt"),
        P("prompt", sample, None, None),
        P("prompt", sample),
        P("prompt", sample, None),
        P(None, sample),
    )
    out_specs = P("prompt", None, sample)
    return jax.shard_map(local, mesh=fine, in_specs=in_specs, out_specs=out_specs, check_vma=False)
```
